32 devices in a mesh: ctx: 16 (over z, y, x), tp: 2 (over core).
Axes of the slice: x: 2, y: 2, z: 4, core: 2. Of those that a mesh axis runs over, the one named last changes fastest.
Arguments:
- query_in: bfloat16 [4096, 8192], P('ctx', 'tp'), may hold values from -6 to 6
- key_in: bfloat16 [4096, 8192], P('ctx', 'tp'), may hold values from -6 to 6
- value_in: bfloat16 [4096, 8192], P('ctx', 'tp'), may hold values from -6 to 6
- out_grad: bfloat16 [4096, 8192], P('ctx', 'tp'), may hold values from -400 to 400
- fill_counts: int32 [16], P('ctx'), may hold values from 192 to 256, as said below
- doc_starts: int32 [4], replicated, may hold values from 0 to 3071, as said below
- feat_taps: bfloat16 [3, 7, 8192], P(None, None, 'tp'), may hold values from -2 to 2
- mix_taps: bfloat16 [512, 128], P('tp'), may hold values from -0.5 to 0.5
- skip_gain: float32 [8192], P('tp'), may hold values from -4 to 4
Outputs:
- hyena_out: bfloat16 [4096, 8192], P('ctx', 'tp')
- query_grad: bfloat16 [4096, 8192], P('ctx', 'tp')
- key_grad: bfloat16 [4096, 8192], P('ctx', 'tp')
- value_grad: bfloat16 [4096, 8192], P('ctx', 'tp')
- mix_grad: float32 [512, 128], P('tp')
- skip_grad: float32 [8192], P('tp')
- feat_grad: float32 [3, 7, 8192], P(None, None, 'tp')
The draws below stay inside these ranges and needn't reach their ends.
Inputs may be any that keep to these rules, and one draw needn't show every extreme that they name: `fill_counts`: entry s is the number of filled slots of shard s; the filled slots are a shard's first ones. Some shard is full. `doc_starts`: strictly increasing; the first entry is 0.
All inputs are finite; a program needn't handle non-finite values.
Results may differ from the reference program's by a relative error of at most 0.0075.
Values may be sent and summed in bfloat16 or wider, within the bound.
No kernel may reach another device: no remote copies, remote signals or barrier semaphores. Data moves between devices by JAX's collectives and lax.ppermute only.
A program may use at most 256 MiB of HBM per device.

```python
import math
import jax
import jax.numpy as jnp
from jax import lax

D = 8192
FILT = 128
SHORT = 7
ROWS = 256
DOCS = 4
SHARDS = 16
TOKENS = 4096
GROUPS = 512
N_TP = 2


def draw_fill_counts(key, part):
    subkeys = jax.random.split(jax.random.fold_in(key, 11), 2)
    counts = jax.random.randint(subkeys[0], (SHARDS,), 3 * ROWS // 4, ROWS + 1, dtype=jnp.int32)
    order = jax.random.permutation(subkeys[1], SHARDS)
    counts = counts.at[order[0]].set(ROWS)
    counts = counts.at[order[1]].set(3 * ROWS // 4)
    return counts.astype(jnp.int32)


def draw_doc_starts(key, part):
    limit = SHARDS * (3 * ROWS // 4)
    picked = jax.random.permutation(jax.random.fold_in(key, 23), limit - 2)[:DOCS - 2] + 1
    picked = jnp.sort(picked.astype(jnp.int32))
    return jnp.concatenate([jnp.zeros((1,), jnp.int32), picked, jnp.full((1,), limit - 1, jnp.int32)]).astype(jnp.int32)


def draw_out_grad(key, part):
    subkeys = jax.random.split(jax.random.fold_in(key, 37), 3)
    row_pos = jnp.arange(TOKENS, dtype=jnp.float32) / TOKENS
    col_pos = jnp.arange(D, dtype=jnp.float32) / D
    row_scale = (1.0 + 2.0 * row_pos) * jnp.exp(jax.random.uniform(subkeys[0], (TOKENS,), jnp.float32, -0.6, 0.6))
    col_scale = (1.0 + 2.0 * col_pos) * jnp.exp(jax.random.uniform(subkeys[1], (D,), jnp.float32, -0.6, 0.6))
    noise = jnp.clip(jax.random.normal(subkeys[2], (TOKENS, D), jnp.float32), -5.0, 5.0)
    return (noise * row_scale[:, None] * col_scale[None, :]).astype(jnp.bfloat16)


def levels(rng, extent, cuts, smallest, top_value):
    loudness, own = 1.0, jax.random.fold_in(rng, 6)
    for axis_at, shards_of in cuts:
        steps = jnp.exp(jax.random.uniform(jax.random.fold_in(own, axis_at), (shards_of,), jnp.float32, smallest / len(cuts), top_value / len(cuts)))
        loudness = loudness * jnp.repeat(steps, extent[axis_at] // shards_of).reshape([-1 if axis == axis_at else 1 for axis in range(len(extent))])
    return loudness


def bell_draw(rng, shape, scale, reach, cuts=(), kind=jnp.bfloat16):
    result = jax.random.normal(rng, shape, jnp.float32) * scale
    if len(cuts) > 0:
        result = levels(rng, shape, cuts, -0.22, 0.18) * result
    return jnp.clip(result, min=-reach, max=reach).astype(kind)


def setup_inputs(seed: int = 0) -> dict:
    streams_of = jax.random.split(jax.random.key(seed), 10)
    query_in = bell_draw(streams_of[0], (TOKENS, D), 1.0, 6.0, ((0, 16), (1, 2)))
    key_in = bell_draw(streams_of[1], (TOKENS, D), 1.0, 6.0, ((0, 16), (1, 2)))
    value_in = bell_draw(streams_of[2], (TOKENS, D), 1.0, 6.0, ((0, 16), (1, 2)))
    out_grad = draw_out_grad(jax.random.fold_in(streams_of[9], 71), 0)
    fill_counts = draw_fill_counts(jax.random.fold_in(streams_of[9], 71), 0)
    doc_starts = draw_doc_starts(jax.random.fold_in(streams_of[9], 71), 0)
    feat_taps = bell_draw(streams_of[6], (3, SHORT, D), SHORT ** -0.5, 2.0, ((2, 2),))
    mix_taps = bell_draw(streams_of[7], (GROUPS, FILT), FILT ** -0.5, 0.5, ((0, 2),))
    skip_gain = bell_draw(streams_of[8], (D,), 1.0, 4.0, ((0, 2),), jnp.float32)
    return {"query_in": query_in, "key_in": key_in, "value_in": value_in, "out_grad": out_grad, "fill_counts": fill_counts, "doc_starts": doc_starts, "feat_taps": feat_taps, "mix_taps": mix_taps, "skip_gain": skip_gain}


def doc_index(positions, doc_starts):
    counted = lax.optimization_barrier(jnp.sum((doc_starts[None, :] <= positions[:, None]).astype(jnp.int32), axis=1))
    return (counted - 1).astype(jnp.int32)

def banded(coeffs, block_rows):
    group_count, filter_len = coeffs.shape
    window = block_rows + filter_len - 1
    padded_row = jnp.concatenate([coeffs, jnp.zeros((group_count, window + 1 - filter_len), coeffs.dtype)], axis=1)
    tiled = jnp.broadcast_to(padded_row[:, None, :], (group_count, block_rows, window + 1))
    tiled = tiled.reshape(group_count, block_rows * (window + 1))
    return tiled[:, :block_rows * window].reshape(group_count, block_rows, window)

def diagonals(products, filter_len):
    group_count, block_rows, window = products.shape
    flat = jnp.concatenate([products.reshape(group_count, block_rows * window), jnp.zeros((group_count, block_rows), products.dtype)], axis=1)
    return lax.optimization_barrier(jnp.sum(flat.reshape(group_count, block_rows, window + 1)[:, :, :filter_len], axis=1))

def contract(form, left, right):
    return jnp.einsum(form, left.astype(jnp.float32), right.astype(jnp.float32))

def featurize(extended, doc_ext, weights):
    short_len = weights.shape[0]
    out_rows = extended.shape[0] - short_len + 1
    doc_out = doc_ext[short_len - 1:]
    accum = jnp.zeros((out_rows, extended.shape[1]), jnp.float32)
    for j in range(short_len):
        offset = short_len - 1 - j
        source = extended[offset:offset + out_rows].astype(jnp.float32)
        same_doc = (doc_out == doc_ext[offset:offset + out_rows])[:, None]
        accum = accum + jnp.where(same_doc, weights[j].astype(jnp.float32) * source, 0.0)
    return accum

def unfeaturize(extended, doc_ext, weights):
    short_len = weights.shape[0]
    out_rows = extended.shape[0] - short_len + 1
    doc_out = doc_ext[:out_rows]
    accum = jnp.zeros((out_rows, extended.shape[1]), jnp.float32)
    for j in range(short_len):
        source = extended[j:j + out_rows].astype(jnp.float32)
        same_doc = (doc_out == doc_ext[j:j + out_rows])[:, None]
        accum = accum + jnp.where(same_doc, weights[j].astype(jnp.float32) * source, 0.0)
    return accum

def feat_grads(extended, doc_ext, grads):
    out_rows = grads.shape[0]
    short_len = extended.shape[0] - out_rows + 1
    doc_out = doc_ext[short_len - 1:]
    pieces = []
    for j in range(short_len):
        offset = short_len - 1 - j
        source = extended[offset:offset + out_rows].astype(jnp.float32)
        same_doc = (doc_out == doc_ext[offset:offset + out_rows])[:, None]
        pieces.append(lax.optimization_barrier(jnp.sum(jnp.where(same_doc, source * grads.astype(jnp.float32), 0.0), axis=0)))
    return jnp.stack(pieces)

def mix_blocks(extended, doc_ext, band, leading):
    group_count, block_rows, window = band.shape
    filter_len = window - block_rows + 1
    channels = extended.shape[1]
    per_group = channels // group_count
    out_rows = extended.shape[0] - filter_len + 1

    def per_block(b):
        first = b * block_rows
        source = lax.dynamic_slice_in_dim(extended, first, window, 0).reshape(window, group_count, per_group)
        doc_src = lax.dynamic_slice_in_dim(doc_ext, first, window, 0)
        doc_out = doc_src[filter_len - 1:] if leading else doc_src[:block_rows]
        matrix = jnp.where((doc_out[:, None] == doc_src[None, :])[None], band, jnp.zeros((), band.dtype))
        return contract('gas,sgc->agc', matrix, source).reshape(block_rows, channels)
    blocks = lax.map(per_block, jnp.arange(out_rows // block_rows, dtype=jnp.int32))
    return blocks.reshape(out_rows, channels)

def grad_blocks(ext_grad, doc_back, ext_mix, doc_long, row_grads, band):
    group_count, block_rows, window = band.shape
    filter_len = window - block_rows + 1
    out_rows, channels = row_grads.shape
    per_group = channels // group_count

    def per_block(b):
        first = b * block_rows
        source = lax.dynamic_slice_in_dim(ext_grad, first, window, 0).reshape(window, group_count, per_group)
        doc_src = lax.dynamic_slice_in_dim(doc_back, first, window, 0)
        matrix = jnp.where((doc_src[:block_rows, None] == doc_src[None, :])[None], band, jnp.zeros((), band.dtype))
        back_rows = contract('gas,sgc->agc', matrix, source).reshape(block_rows, channels)
        mix_src = lax.dynamic_slice_in_dim(ext_mix, first, window, 0).reshape(window, group_count, per_group)
        doc_mix = lax.dynamic_slice_in_dim(doc_long, first, window, 0)
        own_rows = lax.dynamic_slice_in_dim(row_grads, first, block_rows, 0).reshape(block_rows, group_count, per_group)
        products = contract('agc,sgc->gas', own_rows, mix_src)
        products = jnp.where((doc_mix[filter_len - 1:, None] == doc_mix[None, :])[None], products, 0.0)
        return (back_rows, diagonals(products, filter_len))
    back_all, taps_all = lax.map(per_block, jnp.arange(out_rows // block_rows, dtype=jnp.int32))
    return (back_all.reshape(out_rows, channels), lax.optimization_barrier(jnp.sum(taps_all, axis=0))[:, ::-1])

def channel_block(query_in, key_in, value_in, out_grad, feat_taps, mix_taps, skip_gain, doc_ids):
    token_count, channels = query_in.shape
    short_len = feat_taps.shape[1]
    filter_len = mix_taps.shape[1]
    block_rows = math.gcd(ROWS, 128)
    doc_short = jnp.concatenate([jnp.full((short_len - 1,), -2, jnp.int32), doc_ids])
    pad_short = jnp.zeros((short_len - 1, channels), query_in.dtype)
    ext_q = jnp.concatenate([pad_short, query_in], axis=0)
    ext_k = jnp.concatenate([pad_short, key_in], axis=0)
    ext_v = jnp.concatenate([pad_short, value_in], axis=0)
    query = featurize(ext_q, doc_short, feat_taps[0])
    keys = featurize(ext_k, doc_short, feat_taps[1])
    values = featurize(ext_v, doc_short, feat_taps[2])
    mix_in = (keys * values).astype(jnp.bfloat16)
    doc_long = jnp.concatenate([jnp.full((filter_len - 1,), -2, jnp.int32), doc_ids])
    ext_mix = jnp.concatenate([jnp.zeros((filter_len - 1, channels), mix_in.dtype), mix_in], axis=0)
    mixed = mix_blocks(ext_mix, doc_long, banded(mix_taps[:, ::-1], block_rows), True)
    gated = mixed + skip_gain[None, :] * mix_in.astype(jnp.float32)
    hyena_out = (query * gated).astype(jnp.bfloat16)
    grad_f = out_grad.astype(jnp.float32)
    mix_grad_rows = (grad_f * query).astype(jnp.bfloat16)
    query_back = (grad_f * gated).astype(jnp.bfloat16)
    ext_grad = jnp.concatenate([mix_grad_rows, jnp.zeros((filter_len - 1, channels), mix_grad_rows.dtype)], axis=0)
    doc_back = jnp.concatenate([doc_ids, jnp.full((filter_len - 1,), -3, jnp.int32)])
    back_rows, taps_grad = grad_blocks(ext_grad, doc_back, ext_mix, doc_long, mix_grad_rows, banded(mix_taps, block_rows))
    mix_back = back_rows + skip_gain[None, :] * mix_grad_rows.astype(jnp.float32)
    key_back = (mix_back * values).astype(jnp.bfloat16)
    value_back = (mix_back * keys).astype(jnp.bfloat16)
    doc_near = doc_back[:token_count + short_len - 1]
    tail_pad = jnp.zeros((short_len - 1, channels), jnp.bfloat16)
    query_grad = unfeaturize(jnp.concatenate([query_back, tail_pad], axis=0), doc_near, feat_taps[0]).astype(jnp.bfloat16)
    key_grad = unfeaturize(jnp.concatenate([key_back, tail_pad], axis=0), doc_near, feat_taps[1]).astype(jnp.bfloat16)
    value_grad = unfeaturize(jnp.concatenate([value_back, tail_pad], axis=0), doc_near, feat_taps[2]).astype(jnp.bfloat16)
    feat = jnp.stack([feat_grads(ext_q, doc_short, query_back), feat_grads(ext_k, doc_short, key_back), feat_grads(ext_v, doc_short, value_back)])
    skip_part = lax.optimization_barrier(jnp.sum(mix_in.astype(jnp.float32) * mix_grad_rows.astype(jnp.float32), axis=0))
    return (hyena_out, query_grad, key_grad, value_grad, taps_grad, skip_part, feat)

def reference(query_in, key_in, value_in, out_grad, fill_counts, doc_starts, feat_taps, mix_taps, skip_gain):
    starts = (jnp.cumsum(fill_counts) - fill_counts).astype(jnp.int32)
    slot_pos = jnp.arange(ROWS, dtype=jnp.int32)
    is_valid = (slot_pos[None, :] < fill_counts[:, None]).reshape(TOKENS)
    slot_index = jnp.where(is_valid, (starts[:, None] + slot_pos[None, :]).reshape(TOKENS), TOKENS).astype(jnp.int32)
    gather_at = jnp.minimum(slot_index, TOKENS - 1).astype(jnp.int32)
    doc_ids = doc_index(jnp.arange(TOKENS, dtype=jnp.int32), doc_starts)
    channels = D // N_TP

    def to_blocks(source):
        stream = jnp.zeros_like(source).at[slot_index].set(source, mode='drop')
        return stream.reshape(TOKENS, N_TP, channels).transpose(1, 0, 2)

    def from_blocks(blocks):
        stream = blocks.transpose(1, 0, 2).reshape(TOKENS, D)
        return jnp.where(is_valid[:, None], stream[gather_at], jnp.zeros((), stream.dtype))
    feat_blocks = feat_taps.reshape(3, SHORT, N_TP, channels).transpose(2, 0, 1, 3)
    taps_blocks = mix_taps.reshape(N_TP, GROUPS // N_TP, FILT)
    skip_blocks = skip_gain.reshape(N_TP, channels)

    def run_block(operands):
        return channel_block(operands[0], operands[1], operands[2], operands[3], operands[4], operands[5], operands[6], doc_ids)
    results = lax.map(run_block, (to_blocks(query_in), to_blocks(key_in), to_blocks(value_in), to_blocks(out_grad), feat_blocks, taps_blocks, skip_blocks))
    hyena_out = from_blocks(results[0])
    query_grad = from_blocks(results[1])
    key_grad = from_blocks(results[2])
    value_grad = from_blocks(results[3])
    raw_mix = results[4].reshape(GROUPS, FILT)
    raw_skip = results[5].reshape(D)
    raw_feat = results[6].transpose(1, 2, 0, 3).reshape(3, SHORT, D)
    whole_sq = jnp.sum(raw_mix * raw_mix) + jnp.sum(raw_skip * raw_skip) + jnp.sum(raw_feat * raw_feat)
    total_params = GROUPS * FILT + D * (1 + 3 * SHORT)
    factor = lax.rsqrt(whole_sq / total_params + 1e-06)
    return (hyena_out, query_grad, key_grad, value_grad, raw_mix * factor, raw_skip * factor, raw_feat * factor)
```

```python
import functools

import jax
import jax.numpy as jnp
from jax import lax
from jax.experimental import pallas as pl
from jax.experimental.pallas import tpu as pltpu
from jax.sharding import PartitionSpec as P

LANES = 128
PAD = 8
STRIP = 64
CHUNKS = 2
WIDE = 512
BF = jnp.bfloat16
F32 = jnp.float32


def shift(value, axis, steps):
    count = lax.axis_size(axis)
    pairs = [(s, s + steps) for s in range(count) if 0 <= s + steps < count]
    return lax.ppermute(value, axis, pairs)


def iota(shape, dim):
    return lax.broadcasted_iota(jnp.int32, shape, dim)


def fill_dist(scal, docs, dist_ref):
    rows = dist_ref.shape[0]
    pos = iota((rows, LANES), 0)
    start = jnp.full((rows, LANES), -(2**20), jnp.int32)
    for k in range(docs):
        edge = scal[2 + k] - scal[0]
        start = jnp.where(edge <= pos, jnp.maximum(start, edge), start)
    dist_ref[...] = pos - start


def crosses(scal, docs, first, last):
    hit = False
    for k in range(docs):
        edge = scal[2 + k] - scal[0]
        hit = jnp.logical_or(hit, jnp.logical_and(edge > first, edge <= last))
    return hit


def either(cond, body):
    @pl.when(cond)
    def _():
        body(True)

    @pl.when(jnp.logical_not(cond))
    def _():
        body(False)


def featurize_kernel(
    docs, short, scal, q_ref, k_ref, v_ref, og_ref, halo_ref, taps_ref,
    query_ref, keys_ref, values_ref, mix_ref, mgr_ref, tail_ref, head_ref,
    dist, ext, mixed,
):
    rows, width = q_ref.shape
    filled = scal[1]
    edge_rows = tail_ref.shape[0]

    @pl.when(pl.program_id(0) == 0)
    def _():
        fill_dist(scal, docs, dist)

    def tile(t, carry):
        cols = pl.ds(pl.multiple_of(t * LANES, LANES), LANES)
        halo = halo_ref[:, cols].astype(F32)
        for w, ref in enumerate((q_ref, k_ref, v_ref)):
            ext[w, 0:PAD, :] = halo[w * PAD : (w + 1) * PAD]
            ext[w, PAD : PAD + rows, :] = ref[:, cols].astype(F32)
        for r0 in range(0, rows, STRIP):
            span = slice(r0, r0 + STRIP)

            def strip(masked, r0=r0, span=span):
                outs = []
                for w in range(3):
                    acc = None
                    for j in range(short):
                        source = ext[w, PAD + r0 - j : PAD + r0 - j + STRIP, :]
                        term = taps_ref[w * short + j : w * short + j + 1, cols] * source
                        if masked and j:
                            term = jnp.where(dist[span, :] >= j, term, 0.0)
                        acc = term if acc is None else acc + term
                    outs.append(acc)
                query, keys, values = outs
                query_ref[span, cols] = query.astype(BF)
                keys_ref[span, cols] = keys.astype(BF)
                values_ref[span, cols] = values.astype(BF)
                mix = (keys * values).astype(BF)
                mix_ref[span, cols] = mix
                mixed[span, :] = mix.astype(F32)
                valid = iota((STRIP, LANES), 0) + r0 < filled
                mgr = jnp.where(valid, og_ref[span, cols].astype(F32) * query, 0.0).astype(BF)
                mgr_ref[span, cols] = mgr
                if r0 < edge_rows:
                    head_ref[span, cols] = mgr

            either(crosses(scal, docs, r0 - PAD, r0 + STRIP + PAD), strip)
        tail_ref[:, cols] = mixed[pl.ds(filled - edge_rows, edge_rows), :].astype(BF)
        return carry

    lax.fori_loop(0, width // LANES, tile, 0)


def pair_mask(scal, docs, shape, p_dim, p0, s0, taps):
    p = iota(shape, p_dim) + p0
    s = iota(shape, 1 - p_dim) + s0
    lag = p - s
    keep = jnp.where(jnp.logical_and(lag >= 0, lag < taps), 1.0, 0.0)
    for k in range(docs):
        edge = scal[2 + k] - scal[0]
        keep = jnp.where(jnp.logical_and(s < edge, edge <= p), 0.0, keep)
    return keep


def mix_kernel(
    docs, short, per_group, scal, prev_ref, mix_ref, mgr_ref, next_ref, query_ref, keys_ref,
    values_ref, og_ref, q_ref, k_ref, v_ref, halo_ref, hfwd_ref, hrev_ref, skip_ref, *rest,
):
    hyena_ref, qb_ref, kb_ref, vb_ref, head_ref, tapg_ref, feat_ref = rest[-19:-12]
    dist, m_fwd, m_bwd, m_lag, ext, xs, gext, gs, lhs, yacc, bacc, facc = rest[-12:]
    rows, width = mix_ref.shape
    taps = LANES
    blocks = rows // taps
    filled = scal[1]
    groups = LANES // per_group
    square = (taps, taps)

    @pl.when(pl.program_id(0) == 0)
    def _():
        fill_dist(scal, docs, dist)
        for b in range(blocks):
            for half in range(2):
                keep = pair_mask(scal, docs, square, 0, b * taps, (b - 1 + half) * taps, taps)
                m_fwd[b, :, half * taps : (half + 1) * taps] = keep.astype(BF)
                m_lag[b, :, half * taps : (half + 1) * taps] = keep
                keep = pair_mask(scal, docs, square, 1, (b + half) * taps, b * taps, taps)
                m_bwd[b, :, half * taps : (half + 1) * taps] = keep.astype(BF)

    def tile(t, carry):
        cols = pl.ds(pl.multiple_of(t * LANES, LANES), LANES)
        halo = halo_ref[:, cols].astype(F32)
        for w, ref in enumerate((q_ref, k_ref, v_ref)):
            ext[w, 0:PAD, :] = halo[w * PAD : (w + 1) * PAD]
            ext[w, PAD : PAD + rows, :] = ref[:, cols].astype(F32)
        xs[0:taps, :] = prev_ref[:, cols]
        xs[taps : taps + rows, :] = mix_ref[:, cols]
        gext[0:rows, :] = mgr_ref[:, cols].astype(F32)
        gext[rows : rows + taps, :] = jnp.zeros(square, F32)
        gext[pl.ds(filled, taps), :] = next_ref[:, cols].astype(F32)
        gs[...] = gext[...].astype(BF)
        group_of = iota((taps, LANES), 1) // per_group

        for g in range(groups):
            row = t * groups + g
            crev = pltpu.roll(
                jnp.broadcast_to(hrev_ref[pl.ds(row, 1), :], square), 0, 1, stride=1, stride_axis=0
            ).astype(BF)
            cfwd = pltpu.roll(
                jnp.broadcast_to(hfwd_ref[pl.ds(row, 1), :], square), 0, 1, stride=1, stride_axis=0
            ).astype(BF)
            crev2 = jnp.concatenate([crev, crev], axis=1)
            cfwd2 = jnp.concatenate([cfwd, cfwd], axis=1)
            mine = group_of == g
            total = None
            for b in range(blocks):
                out = jnp.dot(
                    crev2 * m_fwd[b], xs[b * taps : (b + 2) * taps, :], preferred_element_type=F32
                )
                here = slice(b * taps, (b + 1) * taps)
                yacc[here, :] = out if g == 0 else jnp.where(mine, out, yacc[here, :])
                out = jnp.dot(
                    cfwd2 * m_bwd[b], gs[b * taps : (b + 2) * taps, :], preferred_element_type=F32
                )
                bacc[here, :] = out if g == 0 else jnp.where(mine, out, bacc[here, :])
                own = jnp.where(mine, mgr_ref[here, cols], jnp.zeros((), BF))
                prod = lax.dot_general(
                    own, xs[b * taps : (b + 2) * taps, :], (((1,), (1,)), ((), ())),
                    preferred_element_type=F32,
                )
                prod = prod * m_lag[b]
                prod = prod[:, :taps] + prod[:, taps:]
                total = prod if total is None else total + prod
            acc = total[0:8, :]
            for i in range(1, taps // 8):
                acc = acc + pltpu.roll(total[8 * i : 8 * i + 8, :], taps - 8 * i, 1)
            sub = iota((8, LANES), 0)
            for bit in (1, 2, 4):
                acc = jnp.where((sub & bit) != 0, pltpu.roll(acc, taps - bit, 1), acc)
            tapg_ref[pl.ds(row, 1), :] = jnp.sum(acc, axis=0, keepdims=True)

        facc[...] = jnp.zeros_like(facc)
        skip = skip_ref[:, cols]
        for r0 in range(0, rows, STRIP):
            span = slice(r0, r0 + STRIP)
            valid = iota((STRIP, LANES), 0) + r0 < filled
            mix = mix_ref[span, cols].astype(F32)
            mgr = mgr_ref[span, cols].astype(F32)
            gated = yacc[span, :] + skip * mix
            back = bacc[span, :] + skip * mgr
            hyena_ref[span, cols] = jnp.where(
                valid, query_ref[span, cols].astype(F32) * gated, 0.0
            ).astype(BF)
            qb = jnp.where(valid, og_ref[span, cols].astype(F32) * gated, 0.0).astype(BF)
            kb = jnp.where(valid, back * values_ref[span, cols].astype(F32), 0.0).astype(BF)
            vb = jnp.where(valid, back * keys_ref[span, cols].astype(F32), 0.0).astype(BF)
            qb_ref[span, cols] = qb
            kb_ref[span, cols] = kb
            vb_ref[span, cols] = vb
            grads = [qb.astype(F32), kb.astype(F32), vb.astype(F32)]
            if r0 == 0:
                for w in range(3):
                    head_ref[w * PAD : (w + 1) * PAD, cols] = grads[w][0:PAD].astype(BF)

            def rows_sum(value):
                return jnp.sum(value.reshape(STRIP // 8, 8, LANES), axis=0)

            last = 3 * short * 8
            facc[last : last + 8, :] += rows_sum(mix * mgr)

            def strip(masked, r0=r0, span=span, grads=grads):
                for w in range(3):
                    for j in range(short):
                        source = ext[w, PAD + r0 - j : PAD + r0 - j + STRIP, :]
                        term = source * grads[w]
                        if masked and j:
                            term = jnp.where(dist[span, :] >= j, term, 0.0)
                        at = (w * short + j) * 8
                        facc[at : at + 8, :] += rows_sum(term)

            either(crosses(scal, docs, r0 - PAD, r0 + STRIP + PAD), strip)
        slots = feat_ref.shape[0] // (width // LANES)
        summed = jnp.sum(facc[...].reshape(slots, 8, LANES), axis=1)
        feat_ref[pl.ds(pl.multiple_of(t * slots, slots), slots), :] = summed
        return carry

    lax.fori_loop(0, width // LANES, tile, 0)


def unfeaturize_kernel(docs, short, scal, qb_ref, kb_ref, vb_ref, halo_ref, taps_ref, *rest):
    outs = rest[-5:-2]
    dist, ext = rest[-2:]
    rows, width = qb_ref.shape
    filled = scal[1]

    @pl.when(pl.program_id(0) == 0)
    def _():
        fill_dist(scal, docs, dist)

    def tile(t, carry):
        cols = pl.ds(pl.multiple_of(t * LANES, LANES), LANES)
        halo = halo_ref[:, cols].astype(F32)
        for w, ref in enumerate((qb_ref, kb_ref, vb_ref)):
            ext[w, 0:rows, :] = ref[:, cols].astype(F32)
            ext[w, pl.ds(filled, PAD), :] = halo[w * PAD : (w + 1) * PAD]
        for r0 in range(0, rows, STRIP):
            span = slice(r0, r0 + STRIP)

            def strip(masked, r0=r0, span=span):
                valid = iota((STRIP, LANES), 0) + r0 < filled
                for w in range(3):
                    acc = None
                    for j in range(short):
                        source = ext[w, r0 + j : r0 + j + STRIP, :]
                        term = taps_ref[w * short + j : w * short + j + 1, cols] * source
                        if masked and j:
                            term = jnp.where(dist[r0 + j : r0 + j + STRIP, :] >= j, term, 0.0)
                        acc = term if acc is None else acc + term
                    outs[w][span, cols] = jnp.where(valid, acc, 0.0).astype(BF)

            either(crosses(scal, docs, r0 - PAD, r0 + STRIP + PAD), strip)
        return carry

    lax.fori_loop(0, width // LANES, tile, 0)


def call(kernel, grid, ins, outs, scratch, args, scal, aliases=None, cost=None):
    specs = pltpu.PrefetchScalarGridSpec(
        num_scalar_prefetch=1, grid=grid, in_specs=[s for s in ins],
        out_specs=[s for s, _ in outs], scratch_shapes=scratch,
    )
    return pl.pallas_call(
        kernel, grid_spec=specs, out_shape=[o for _, o in outs],
        input_output_aliases=aliases or {},
        compiler_params=pltpu.CompilerParams(
            dimension_semantics=("arbitrary",), vmem_limit_bytes=56 * 1024 * 1024
        ),
        cost_estimate=cost,
    )(scal, *args)


def shards(
    query_in, key_in, value_in, out_grad, fill_counts, doc_starts, feat_taps, mix_taps, skip_gain
):
    rows, channels = query_in.shape
    short = feat_taps.shape[1]
    groups, taps = mix_taps.shape
    docs = doc_starts.shape[0]
    per_group = channels // groups
    shard_count, mine = lax.axis_size("ctx"), lax.axis_index("ctx")
    filled = fill_counts[0]

    def tail_rows(source):
        return lax.dynamic_slice_in_dim(source, filled - PAD, PAD, 0)

    tails = jnp.concatenate([tail_rows(s) for s in (query_in, key_in, value_in)], axis=0)
    halo = shift(tails, "ctx", 1)
    counts = lax.all_gather(fill_counts, "ctx", tiled=True)
    first = jnp.sum(jnp.where(jnp.arange(shard_count) < mine, counts, 0))
    scal = jnp.concatenate([first[None], fill_counts, doc_starts]).astype(jnp.int32)

    slots = 3 * short + 1
    slots = slots + (-slots) % 8
    taps_all = jnp.pad(feat_taps.reshape(3 * short, channels).astype(F32), ((0, slots - 3 * short), (0, 0)))
    hfwd = mix_taps.astype(F32)
    hrev = jnp.concatenate([hfwd[:, :1], hfwd[:, :0:-1]], axis=1)
    skip = skip_gain[None, :]

    chunks = CHUNKS
    per_chunk = channels // chunks
    wide = min(WIDE, per_chunk)
    steps = per_chunk // wide
    tiles = wide // LANES
    bf = lambda *shape: jax.ShapeDtypeStruct(shape, BF)
    f32 = lambda *shape: jax.ShapeDtypeStruct(shape, F32)

    def cols(height, offset=0):
        return pl.BlockSpec((height, wide), lambda i, s: (0, i + offset))

    featured, sent_mix, sent_grad = [], [], []
    for c in range(chunks):
        off = c * steps
        full = cols(rows, off)
        outs = call(
            functools.partial(featurize_kernel, docs, short), (steps,),
            [full] * 4 + [cols(3 * PAD, off), cols(slots, off)],
            [(cols(rows), bf(rows, per_chunk))] * 5 + [(cols(taps), bf(taps, per_chunk))] * 2,
            [
                pltpu.VMEM((rows, LANES), jnp.int32),
                pltpu.VMEM((3, PAD + rows, LANES), F32),
                pltpu.VMEM((rows, LANES), F32),
            ],
            (query_in, key_in, value_in, out_grad, halo, taps_all), scal,
            cost=pl.CostEstimate(flops=50 * rows * per_chunk, bytes_accessed=20 * rows * per_chunk, transcendentals=0),
        )
        featured.append(outs)
        sent_mix.append(shift(outs[5], "ctx", 1))
        sent_grad.append(shift(outs[6], "ctx", -1))

    hyena = None
    backs, sent_back, tap_grads, feat_grads = [], [], [], []
    blocks = rows // taps
    for c in range(chunks):
        off = c * steps
        query, keys, values, mix, mgr = featured[c][:5]
        full = cols(rows, off)
        ins = [cols(taps), cols(rows), cols(rows), cols(taps)] + [cols(rows)] * 3 + [full] * 4
        ins += [cols(3 * PAD, off)]
        gspec = pl.BlockSpec((wide // per_group, taps), lambda i, s, off=off: (i + off, 0))
        ins += [gspec, gspec, cols(1, off)]
        args = [sent_mix[c], mix, mgr, sent_grad[c], query, keys, values, out_grad]
        args += [query_in, key_in, value_in, halo, hfwd, hrev, skip]
        aliases = None
        if hyena is not None:
            ins.append(pl.BlockSpec(memory_space=pl.ANY))
            args.append(hyena)
            aliases = {len(args): 0}
        outs = call(
            functools.partial(mix_kernel, docs, short, per_group), (steps,), ins,
            [(full, bf(rows, channels))]
            + [(cols(rows), bf(rows, per_chunk))] * 3
            + [(cols(3 * PAD), bf(3 * PAD, per_chunk))]
            + [
                (pl.BlockSpec((wide // per_group, taps), lambda i, s: (i, 0)), f32(per_chunk // per_group, taps)),
                (pl.BlockSpec((tiles * slots, LANES), lambda i, s: (i, 0)), f32(per_chunk // LANES * slots, LANES)),
            ],
            [
                pltpu.VMEM((rows, LANES), jnp.int32),
                pltpu.VMEM((blocks, taps, 2 * taps), BF),
                pltpu.VMEM((blocks, taps, 2 * taps), BF),
                pltpu.VMEM((blocks, taps, 2 * taps), F32),
                pltpu.VMEM((3, PAD + rows, LANES), F32),
                pltpu.VMEM((rows + taps, LANES), BF),
                pltpu.VMEM((rows + taps, LANES), F32),
                pltpu.VMEM((rows + taps, LANES), BF),
                pltpu.VMEM((8, LANES), BF),
                pltpu.VMEM((rows, LANES), F32),
                pltpu.VMEM((rows, LANES), F32),
                pltpu.VMEM((8 * slots, LANES), F32),
            ],
            args, scal, aliases,
            cost=pl.CostEstimate(flops=2000 * rows * per_chunk, bytes_accessed=40 * rows * per_chunk, transcendentals=0),
        )
        hyena = outs[0]
        backs.append(outs[1:4])
        sent_back.append(shift(outs[4], "ctx", -1))
        tap_grads.append(outs[5])
        feat_grads.append(outs[6])

    grads = None
    for c in range(chunks):
        off = c * steps
        ins = [cols(rows)] * 3 + [cols(3 * PAD), cols(slots, off)]
        args = list(backs[c]) + [sent_back[c], taps_all]
        aliases = None
        if grads is not None:
            for w in range(3):
                ins.append(pl.BlockSpec(memory_space=pl.ANY))
                args.append(grads[w])
            aliases = {len(args) - 2 + w: w for w in range(3)}
        grads = call(
            functools.partial(unfeaturize_kernel, docs, short), (steps,), ins,
            [(cols(rows, off), bf(rows, channels))] * 3,
            [
                pltpu.VMEM((rows + 2 * PAD, LANES), jnp.int32),
                pltpu.VMEM((3, rows + 2 * PAD, LANES), F32),
            ],
            args, scal, aliases,
            cost=pl.CostEstimate(flops=50 * rows * per_chunk, bytes_accessed=12 * rows * per_chunk, transcendentals=0),
        )

    payload = jnp.concatenate(feat_grads + tap_grads, axis=0)
    lines = payload.shape[0]
    extra = (-lines) % shard_count
    payload = jnp.pad(payload, ((0, extra), (0, 0))).astype(BF)
    share = payload.shape[0] // shard_count
    pieces = lax.all_to_all(payload, "ctx", 0, 0, tiled=True)
    summed = jnp.sum(pieces.reshape(shard_count, share, LANES).astype(F32), axis=0).astype(BF)
    spread = jnp.broadcast_to(summed[None], (shard_count, share, LANES)).reshape(-1, LANES)
    whole = lax.all_to_all(spread, "ctx", 0, 0, tiled=True)[:lines].astype(F32)
    total_params = (groups * taps + channels * (1 + 3 * short)) * lax.axis_size("tp")
    whole_sq = lax.psum(jnp.sum(whole * whole), "tp")
    factor = lax.rsqrt(whole_sq / total_params + 1e-06)
    scaled = whole * factor
    split = channels // LANES * slots
    mix_part = scaled[split:]
    mix_out = jnp.concatenate([mix_part[:, :1], mix_part[:, :0:-1]], axis=1)
    feat = scaled[:split].reshape(channels // LANES, slots, LANES).transpose(1, 0, 2).reshape(slots, channels)
    feat_out = feat[: 3 * short].reshape(3, short, channels)
    skip_out = feat[3 * short]
    return (hyena, grads[0], grads[1], grads[2], mix_out, skip_out, feat_out)


def solution(mesh):
    stream = P("ctx", "tp")
    in_specs = (
        stream, stream, stream, stream, P("ctx"), P(), P(None, None, "tp"), P("tp", None), P("tp"),
    )
    out_specs = (stream, stream, stream, stream, P("tp", None), P("tp"), P(None, None, "tp"))
    return jax.shard_map(shards, mesh=mesh, in_specs=in_specs, out_specs=out_specs, check_vma=False)
```

```python
import functools
import math

import jax
import jax.numpy as jnp
from jax import lax
from jax.experimental import pallas as pl
from jax.experimental.pallas import tpu as pltpu
from jax.sharding import PartitionSpec as P


LANES = 128
PAD = 8
STRIP = 64
EARLY = 3
WIDE = 512
BF = jnp.bfloat16
F32 = jnp.float32


def shift(value, axis, steps):
    count = lax.axis_size(axis)
    pairs = [(s, s + steps) for s in range(count) if 0 <= s + steps < count]
    return lax.ppermute(value, axis, pairs)


def iota(shape, dim):
    return lax.broadcasted_iota(jnp.int32, shape, dim)


class Layout:
    def __init__(self, firsts, facts):
        self.firsts, self.facts = firsts, facts

    def __getitem__(self, at):
        return self.facts[at] if at else self.firsts[self.facts[0]]


def fill_dist(scal, docs, dist_ref):
    rows = dist_ref.shape[0]
    pos = iota((rows, LANES), 0)
    start = jnp.full((rows, LANES), -(2**20), jnp.int32)
    for k in range(docs):
        edge = scal[2 + k] - scal[0]
        start = jnp.where(edge <= pos, jnp.maximum(start, edge), start)
    dist_ref[...] = pos - start


def crosses(scal, docs, first, last):
    hit = False
    for k in range(docs):
        edge = scal[2 + k] - scal[0]
        hit = jnp.logical_or(hit, jnp.logical_and(edge > first, edge <= last))
    return hit


def either(cond, body):
    @pl.when(cond)
    def _():
        body(True)

    @pl.when(jnp.logical_not(cond))
    def _():
        body(False)


def featurize_kernel(
    docs, short, firsts, facts, q_ref, k_ref, v_ref, og_ref, halo_ref, taps_ref,
    query_ref, keys_ref, values_ref, mix_ref, mgr_ref, tail_ref, head_ref,
    dist, ext, mixed,
):
    scal = Layout(firsts, facts)
    rows, width = q_ref.shape
    filled = scal[1]
    edge_rows = tail_ref.shape[0]

    @pl.when(pl.program_id(0) == 0)
    def _():
        fill_dist(scal, docs, dist)

    def tile(t, carry):
        cols = pl.ds(pl.multiple_of(t * LANES, LANES), LANES)
        taps_of = [taps_ref[w, :, cols].astype(F32) for w in range(3)]
        halo = halo_ref[:, cols].astype(F32)
        for w, ref in enumerate((q_ref, k_ref, v_ref)):
            ext[w, 0:PAD, :] = halo[w * PAD : (w + 1) * PAD]
            ext[w, PAD : PAD + rows, :] = ref[:, cols].astype(F32)
        for r0 in range(0, rows, STRIP):
            span = slice(r0, r0 + STRIP)

            def strip(masked, r0=r0, span=span):
                outs = []
                for w in range(3):
                    acc = None
                    for j in range(short):
                        source = ext[w, PAD + r0 - j : PAD + r0 - j + STRIP, :]
                        term = taps_of[w][j : j + 1, :] * source
                        if masked and j:
                            term = jnp.where(dist[span, :] >= j, term, 0.0)
                        acc = term if acc is None else acc + term
                    outs.append(acc)
                query, keys, values = outs
                query_ref[span, cols] = query.astype(BF)
                keys_ref[span, cols] = keys.astype(BF)
                values_ref[span, cols] = values.astype(BF)
                mix = (keys * values).astype(BF)
                mix_ref[span, cols] = mix
                mixed[span, :] = mix.astype(F32)
                valid = iota((STRIP, LANES), 0) + r0 < filled
                mgr = jnp.where(valid, og_ref[span, cols].astype(F32) * query, 0.0).astype(BF)
                mgr_ref[span, cols] = mgr
                if r0 < edge_rows:
                    head_ref[span, cols] = mgr

            either(crosses(scal, docs, r0 - PAD, r0 + STRIP + PAD), strip)
        tail_ref[:, cols] = mixed[pl.ds(filled - edge_rows, edge_rows), :].astype(BF)
        return carry

    lax.fori_loop(0, width // LANES, tile, 0)


def pair_mask(scal, docs, shape, p_dim, p0, s0, taps):
    p = iota(shape, p_dim) + p0
    s = iota(shape, 1 - p_dim) + s0
    lag = p - s
    keep = jnp.where(jnp.logical_and(lag >= 0, lag < taps), 1.0, 0.0)
    for k in range(docs):
        edge = scal[2 + k] - scal[0]
        keep = jnp.where(jnp.logical_and(s < edge, edge <= p), 0.0, keep)
    return keep


def mix_kernel(
    docs, short, per_group, firsts, facts, prev_ref, mix_ref, mgr_ref, next_ref, query_ref, keys_ref,
    values_ref, og_ref, q_ref, k_ref, v_ref, halo_ref, hfwd_ref, hrev_ref, skip_ref, *rest,
):
    hyena_ref, sums_ref, head_ref, qb_ref, kb_ref, vb_ref = rest[-18:-12]
    m_fwd, m_bwd, m_lag, ext, xs, gext, gs, yacc, bacc, facc, back_rows, tacc = rest[-12:]
    scal = Layout(firsts, facts)
    rows, width = mix_ref.shape
    taps = LANES
    blocks = rows // taps
    filled = scal[1]
    groups = LANES // per_group
    square = (taps, taps)

    @pl.when(pl.program_id(0) == 0)
    def _():
        facc[...] = jnp.zeros_like(facc)
        for end in (0, PAD + rows):
            back_rows[:, end : end + PAD, :] = jnp.zeros((3, PAD, LANES), F32)
        for end in (0, 2 * PAD + rows):
            ext[:, :, end : end + PAD, :] = jnp.zeros((2, 3, PAD, LANES), F32)
        for b in range(blocks):
            for half in range(2):
                keep = pair_mask(scal, docs, square, 0, b * taps, (b - 1 + half) * taps, taps)
                m_fwd[b, :, half * taps : (half + 1) * taps] = keep.astype(BF)
                m_lag[b] = keep if half == 0 else m_lag[b] + keep
                keep = pair_mask(scal, docs, square, 1, (b + half) * taps, b * taps, taps)
                m_bwd[b, :, half * taps : (half + 1) * taps] = keep.astype(BF)

    piece = rows // groups
    count = width // LANES
    skips = 3 * short * 8

    def columns(t):
        return pl.ds(pl.multiple_of(t * LANES, LANES), LANES)

    def setup(t, slot):
        cols = columns(t)
        halo = halo_ref[:, cols].astype(F32)
        for w, ref in enumerate((q_ref, k_ref, v_ref)):
            ext[slot, w, PAD : 2 * PAD, :] = halo[w * PAD : (w + 1) * PAD]
            ext[slot, w, 2 * PAD : 2 * PAD + rows, :] = ref[:, cols].astype(F32)
        xs[0:taps, :] = prev_ref[:, cols]
        xs[taps : taps + rows, :] = mix_ref[:, cols]
        gext[0:rows, :] = mgr_ref[:, cols].astype(F32)
        gext[rows : rows + taps, :] = jnp.zeros(square, F32)
        gext[pl.ds(filled, taps), :] = next_ref[:, cols].astype(F32)
        gs[...] = gext[...].astype(BF)

    def circulant(ref, row):
        line = jnp.broadcast_to(ref[pl.ds(row, 1), :], square)
        return pltpu.roll(line, 0, 1, stride=1, stride_axis=0).astype(BF)

    def group(t, slot, g):
        lane_group = iota((taps, LANES), 1) // per_group
        tri = iota(square, 0) >= iota(square, 1)
        sub = iota((8, LANES), 0)
        row = t * groups + g
        mine = lane_group == g
        crev, cfwd = circulant(hrev_ref, row), circulant(hfwd_ref, row)
        crev2 = jnp.concatenate([crev, crev], axis=1)
        cfwd2 = jnp.concatenate([cfwd, cfwd], axis=1)
        total = None
        for b in range(blocks):
            here = slice(b * taps, (b + 1) * taps)
            window = slice(b * taps, (b + 2) * taps)
            out = jnp.dot(crev2 * m_fwd[b], xs[window, :], preferred_element_type=F32)
            pltpu.store(yacc.at[slot, here, :], out, mask=mine)
            out = jnp.dot(cfwd2 * m_bwd[b], gs[window, :], preferred_element_type=F32)
            pltpu.store(bacc.at[slot, here, :], out, mask=mine)
            own = jnp.where(mine, mgr_ref[here, columns(t)], jnp.zeros((), BF))
            prod = lax.dot_general(
                own, xs[window, :], (((1,), (1,)), ((), ())), preferred_element_type=F32
            )
            prod = jnp.where(tri, prod[:, taps:], prod[:, :taps]) * m_lag[b]
            total = prod if total is None else total + prod
        acc = total[0:8, :]
        for i in range(1, taps // 8):
            acc = acc + pltpu.roll(total[8 * i : 8 * i + 8, :], taps - 8 * i, 1)
        for bit in (1, 2, 4):
            acc = jnp.where((sub & bit) != 0, pltpu.roll(acc, taps - bit, 1), acc)
        tacc[slot, g : g + 1, :] = jnp.sum(acc, axis=0, keepdims=True)

    def rows_sum(value):
        return jnp.sum(value.reshape(piece // 8, 8, LANES), axis=0)

    def finish_rows(t, slot, r0):
        cols = columns(t)
        span = slice(r0, r0 + piece)

        def gather(at, value):
            if r0:
                facc[at : at + 8, :] += value
            else:
                facc[at : at + 8, :] = value

        valid = iota((piece, LANES), 0) + r0 < filled
        skip = skip_ref[:, cols]
        mix = mix_ref[span, cols].astype(F32)
        mgr = mgr_ref[span, cols].astype(F32)
        gated = yacc[slot, span, :] + skip * mix
        back = bacc[slot, span, :] + skip * mgr
        gather(skips, rows_sum(mix * mgr))
        hyena_ref[span, cols] = jnp.where(
            valid, query_ref[span, cols].astype(F32) * gated, 0.0
        ).astype(BF)
        out_refs = (qb_ref, kb_ref, vb_ref)
        factors = (og_ref, values_ref, keys_ref)
        for w, (out_ref, ref, value) in enumerate(zip(out_refs, factors, (gated, back, back))):
            rounded = jnp.where(valid, ref[span, cols].astype(F32) * value, 0.0).astype(BF)
            out_ref[span, cols] = rounded
            grad = rounded.astype(F32)
            back_rows[w, PAD + r0 : PAD + r0 + piece, :] = grad
            if r0 == 0:
                head_ref[w * PAD : (w + 1) * PAD, cols] = grad[0:PAD].astype(BF)
            for j in range(short):
                source = ext[slot, w, 2 * PAD + r0 - j : 2 * PAD + r0 - j + piece, :]
                gather((w * short + j) * 8, rows_sum(source * grad))

    def finish_sums(t, slot):
        for k in range(docs):
            edge = scal[2 + k] - scal[0]

            @pl.when(jnp.logical_and(edge > -PAD, edge < rows))
            def _(k=k, edge=edge):
                size = scal[3 + k] - scal[2 + k] if k + 1 < docs else rows
                line = iota((PAD, LANES), 0)
                for w in range(3):
                    grad = back_rows[w, pl.ds(PAD + edge, PAD), :]
                    for j in range(1, short):
                        source = ext[slot, w, pl.ds(2 * PAD + edge - j, PAD), :]
                        drop = jnp.where(line < jnp.minimum(size, j), source * grad, 0.0)
                        at = (w * short + j) * 8
                        facc[at : at + 8, :] -= drop

        lines = sums_ref.shape[0] // count
        summed = jnp.sum(facc[...].reshape(lines - groups, 8, LANES), axis=1)
        packed = jnp.concatenate([summed, tacc[slot]], axis=0).astype(BF)
        sums_ref[pl.ds(pl.multiple_of(t * lines, lines), lines), :] = packed

    def tile(t, carry):
        slot = t % 2
        before = jnp.maximum(t - 1, 0)
        setup(t, slot)
        for g in range(groups):
            group(t, slot, g)
            finish_rows(before, 1 - slot, g * piece)
        finish_sums(before, 1 - slot)
        return carry

    lax.fori_loop(0, count, tile, 0)
    for g in range(groups):
        finish_rows(count - 1, (count - 1) % 2, g * piece)
    finish_sums(count - 1, (count - 1) % 2)


def unfeaturize_kernel(
    docs, short, firsts, facts, qb_ref, kb_ref, vb_ref, halo_ref, taps_ref, *rest
):
    outs = rest[-5:-2]
    dist, ext = rest[-2:]
    scal = Layout(firsts, facts)
    rows, width = qb_ref.shape
    filled = scal[1]

    @pl.when(pl.program_id(0) == 0)
    def _():
        fill_dist(scal, docs, dist)

    def tile(t, carry):
        cols = pl.ds(pl.multiple_of(t * LANES, LANES), LANES)
        taps_of = [taps_ref[w, :, cols].astype(F32) for w in range(3)]
        halo = halo_ref[:, cols].astype(F32)
        for w, ref in enumerate((qb_ref, kb_ref, vb_ref)):
            ext[w, 0:rows, :] = ref[:, cols].astype(F32)
            ext[w, pl.ds(filled, PAD), :] = halo[w * PAD : (w + 1) * PAD]
        for r0 in range(0, rows, STRIP):
            span = slice(r0, r0 + STRIP)

            def strip(masked, r0=r0, span=span):
                valid = iota((STRIP, LANES), 0) + r0 < filled
                for w in range(3):
                    acc = None
                    for j in range(short):
                        source = ext[w, r0 + j : r0 + j + STRIP, :]
                        term = taps_of[w][j : j + 1, :] * source
                        if masked and j:
                            term = jnp.where(dist[r0 + j : r0 + j + STRIP, :] >= j, term, 0.0)
                        acc = term if acc is None else acc + term
                    outs[w][span, cols] = jnp.where(valid, acc, 0.0).astype(BF)

            either(crosses(scal, docs, r0 - PAD, r0 + STRIP + PAD), strip)
        return carry

    lax.fori_loop(0, width // LANES, tile, 0)


def call(kernel, grid, ins, outs, scratch, args, scal, aliases=None, cost=None):
    specs = pltpu.PrefetchScalarGridSpec(
        num_scalar_prefetch=2, grid=grid, in_specs=[s for s in ins],
        out_specs=[s for s, _ in outs], scratch_shapes=scratch,
    )
    return pl.pallas_call(
        kernel, grid_spec=specs, out_shape=[o for _, o in outs],
        input_output_aliases=aliases or {},
        compiler_params=pltpu.CompilerParams(
            dimension_semantics=("arbitrary",), vmem_limit_bytes=56 * 1024 * 1024
        ),
        cost_estimate=cost,
    )(*scal, *args)


def shards(
    query_in, key_in, value_in, out_grad, fill_counts, doc_starts, feat_taps, mix_taps, skip_gain
):
    rows, channels = query_in.shape
    short = feat_taps.shape[1]
    groups, taps = mix_taps.shape
    docs = doc_starts.shape[0]
    per_group = channels // groups
    shard_count, mine = lax.axis_size("ctx"), lax.axis_index("ctx")
    filled = fill_counts[0]

    def tail_rows(source):
        return lax.dynamic_slice_in_dim(source, filled - PAD, PAD, 0)

    tails = jnp.concatenate([tail_rows(s) for s in (query_in, key_in, value_in)], axis=0)
    halo = shift(tails, "ctx", 1)
    later = jnp.arange(shard_count, dtype=jnp.int32) > mine
    firsts = lax.psum(jnp.where(later, filled, 0).astype(jnp.int32), "ctx")
    facts = jnp.concatenate([mine[None].astype(jnp.int32), fill_counts, doc_starts])
    scal = (firsts, facts)

    slots = 3 * short + 1
    slots = slots + (-slots) % 8
    hfwd = mix_taps.astype(F32)
    hrev = jnp.concatenate([hfwd[:, :1], hfwd[:, :0:-1]], axis=1)
    skip = skip_gain[None, :]

    tile_count = channels // LANES
    early = max(1, tile_count * EARLY // 8)
    sizes = [early * LANES, (tile_count - early) * LANES]
    starts = [0, early * LANES]
    wide = math.gcd(math.gcd(sizes[0], sizes[1]), WIDE)
    tiles = wide // LANES
    bf = lambda *shape: jax.ShapeDtypeStruct(shape, BF)

    def cols(height, offset=0):
        return pl.BlockSpec((height, wide), lambda i, *s: (0, i + offset))

    def taps_spec(offset):
        return pl.BlockSpec((3, short, wide), lambda i, *s: (0, 0, i + offset))

    featured, sent_mix, sent_grad = [], [], []
    for c, per_chunk in enumerate(sizes):
        off, steps = starts[c] // wide, per_chunk // wide
        full = cols(rows, off)
        outs = call(
            functools.partial(featurize_kernel, docs, short), (steps,),
            [full] * 4 + [cols(3 * PAD, off), taps_spec(off)],
            [(cols(rows), bf(rows, per_chunk))] * 5 + [(cols(taps), bf(taps, per_chunk))] * 2,
            [
                pltpu.VMEM((rows, LANES), jnp.int32),
                pltpu.VMEM((3, PAD + rows, LANES), F32),
                pltpu.VMEM((rows, LANES), F32),
            ],
            (query_in, key_in, value_in, out_grad, halo, feat_taps), scal,
            cost=pl.CostEstimate(flops=50 * rows * per_chunk, bytes_accessed=20 * rows * per_chunk, transcendentals=0),
        )
        featured.append(outs)
        sent_mix.append(shift(outs[5], "ctx", 1))
        sent_grad.append(shift(outs[6], "ctx", -1))

    hyena = sums = heads = None
    backs = []
    lines = slots + LANES // per_group
    blocks = rows // taps
    for c, per_chunk in enumerate(sizes):
        off, steps = starts[c] // wide, per_chunk // wide
        query, keys, values, mix, mgr = featured[c][:5]
        full = cols(rows, off)
        ins = [cols(taps), cols(rows), cols(rows), cols(taps)] + [cols(rows)] * 3 + [full] * 4
        ins += [cols(3 * PAD, off)]
        gspec = pl.BlockSpec((wide // per_group, taps), lambda i, *s, off=off: (i + off, 0))
        ins += [gspec, gspec, cols(1, off)]
        args = [sent_mix[c], mix, mgr, sent_grad[c], query, keys, values, out_grad]
        args += [query_in, key_in, value_in, halo, hfwd, hrev, skip]
        aliases = None
        if hyena is not None:
            ins += [pl.BlockSpec(memory_space=pl.ANY)] * 3
            args += [hyena, sums, heads]
            aliases = {len(args) - 1: 0, len(args): 1, len(args) + 1: 2}
        outs = call(
            functools.partial(mix_kernel, docs, short, per_group), (steps,), ins,
            [
                (full, bf(rows, channels)),
                (
                    pl.BlockSpec((tiles * lines, LANES), lambda i, *s, off=off: (i + off, 0)),
                    bf(channels // LANES * lines, LANES),
                ),
                (cols(3 * PAD, off), bf(3 * PAD, channels)),
            ]
            + [(cols(rows), bf(rows, per_chunk))] * 3,
            [
                pltpu.VMEM((blocks, taps, 2 * taps), BF),
                pltpu.VMEM((blocks, taps, 2 * taps), BF),
                pltpu.VMEM((blocks, taps, taps), F32),
                pltpu.VMEM((2, 3, 3 * PAD + rows, LANES), F32),
                pltpu.VMEM((rows + taps, LANES), BF),
                pltpu.VMEM((rows + taps, LANES), F32),
                pltpu.VMEM((rows + taps, LANES), BF),
                pltpu.VMEM((2, rows, LANES), F32),
                pltpu.VMEM((2, rows, LANES), F32),
                pltpu.VMEM((8 * slots, LANES), F32),
                pltpu.VMEM((3, rows + 2 * PAD, LANES), F32),
                pltpu.VMEM((2, LANES // per_group, LANES), F32),
            ],
            args, scal, aliases,
            cost=pl.CostEstimate(flops=2000 * rows * per_chunk, bytes_accessed=40 * rows * per_chunk, transcendentals=0),
        )
        hyena, sums, heads = outs[:3]
        backs.append(outs[3:6])

    next_heads = shift(heads, "ctx", -1)
    grads = None
    for c, per_chunk in enumerate(sizes):
        off, steps = starts[c] // wide, per_chunk // wide
        ins = [cols(rows)] * 3 + [cols(3 * PAD, off), taps_spec(off)]
        args = list(backs[c]) + [next_heads, feat_taps]
        aliases = None
        if grads is not None:
            for w in range(3):
                ins.append(pl.BlockSpec(memory_space=pl.ANY))
                args.append(grads[w])
            aliases = {len(args) - 1 + w: w for w in range(3)}
        grads = call(
            functools.partial(unfeaturize_kernel, docs, short), (steps,), ins,
            [(cols(rows, off), bf(rows, channels))] * 3,
            [
                pltpu.VMEM((rows + 2 * PAD, LANES), jnp.int32),
                pltpu.VMEM((3, rows + 2 * PAD, LANES), F32),
            ],
            args, scal, aliases,
            cost=pl.CostEstimate(flops=50 * rows * per_chunk, bytes_accessed=12 * rows * per_chunk, transcendentals=0),
        )

    height = sums.shape[0]
    extra = (-height) % shard_count
    payload = jnp.pad(sums, ((0, extra), (0, 0))) if extra else sums
    share = payload.shape[0] // shard_count
    pieces = lax.all_to_all(payload, "ctx", 0, 0, tiled=True)
    summed = jnp.sum(pieces.reshape(shard_count, share, LANES).astype(F32), axis=0).astype(BF)
    spread = jnp.broadcast_to(summed[None], (shard_count, share, LANES)).reshape(-1, LANES)
    whole = lax.all_to_all(spread, "ctx", 0, 0, tiled=True)[:height].astype(F32)
    total_params = (groups * taps + channels * (1 + 3 * short)) * lax.axis_size("tp")
    whole_sq = lax.psum(jnp.sum(whole * whole), "tp")
    factor = lax.rsqrt(whole_sq / total_params + 1e-06)
    scaled = (whole * factor).reshape(channels // LANES, lines, LANES)
    mix_part = scaled[:, slots:].reshape(groups, taps)
    mix_out = jnp.concatenate([mix_part[:, :1], mix_part[:, :0:-1]], axis=1)
    feat = scaled[:, : 3 * short + 1].transpose(1, 0, 2).reshape(3 * short + 1, channels)
    feat_out = feat[: 3 * short].reshape(3, short, channels)
    skip_out = feat[3 * short]
    return (hyena, grads[0], grads[1], grads[2], mix_out, skip_out, feat_out)


def solution(mesh):
    stream = P("ctx", "tp")
    in_specs = (
        stream, stream, stream, stream, P("ctx"), P(), P(None, None, "tp"), P("tp", None), P("tp"),
    )
    out_specs = (stream, stream, stream, stream, P("tp", None), P("tp"), P(None, None, "tp"))
    return jax.shard_map(
        shards, mesh=mesh, in_specs=in_specs, out_specs=out_specs,
        check_vma=False,
    )
```
